32 devices in a mesh: tok: 16 (over z, x, core), exp: 2 (over y).
Axes of the slice: x: 2, y: 2, z: 4, core: 2. Of those that a mesh axis runs over, the one named last changes fastest.
Arguments:
- tokens: bfloat16 [12288, 4096], P('tok'), may hold values from -6 to 6
- route_ids: int32 [12288, 8], P('tok'), may hold values from 0 to 127, all different within a row; in each aligned block of 768 rows (0 to 767, 768 to 1535, ...) at most 128 rows name the same one
- whiten: bfloat16 [4, 4096, 4096], P('exp', 'tok'), may hold values from -0.09375 to 0.09375
- deltas: bfloat16 [4, 4096, 1536], P('exp', 'tok'), may hold values from -6 to 6
- basis: bfloat16 [4096, 768], P('exp'), may hold values from -0.09375 to 0.09375
Outputs:
- gram: float32 [4096, 1, 4096], P('tok', None, 'exp')
- coefficients: float32 [768, 4, 1536], P('tok', 'exp')
- basis_gram: float32 [768, 768], P('tok')
The draws below stay inside these ranges and needn't reach their ends.
Inputs may be any that keep to these rules, and one draw needn't show every extreme that they name: `route_ids`: each row names 8 different experts; among the rows of one device (aligned blocks of 768 rows) no expert is named by more than 128 rows.
All inputs are finite; a program needn't handle non-finite values.
Results may differ from the reference program's by a relative error of at most 0.0029.
Values may be sent and summed in bfloat16 or wider, within the bound.
No kernel may reach another device: no remote copies, remote signals or barrier semaphores. Data moves between devices by JAX's collectives and lax.ppermute only.
A program may use at most 128 MiB of HBM per device.

```python
import math
import jax
import jax.numpy as jnp
import numpy as np
from jax import lax

D = 4096
H = 1536
NROUTE = 128
TOP = 8
R = 768
GRAM_EXP = 1
CAP = 128
TOK_DEV = 768
TOKENS = 12288
EXPERTS = 4


def steps_of(key, shape, pieces, least, largest):
    gain, own = 1.0, jax.random.fold_in(key, 6)
    for axis_at, parts in pieces:
        heights = jnp.exp(jax.random.uniform(jax.random.fold_in(own, axis_at), (parts,), jnp.float32, least / len(pieces), largest / len(pieces)))
        gain = gain * jnp.repeat(heights, shape[axis_at] // parts).reshape([-1 if axis == axis_at else 1 for axis in range(len(shape))])
    return gain


def deal_out(rng, own, number, rows, count, top, most, skew):
    ranking = jax.random.permutation(rng, count)
    heavy_load, common = portions_of(count, rows * top, most, skew, True), portions_of(count, rows * top, most, skew, False)
    places = jnp.arange(count)

    def named(lengths, offset_by):
        used = int((lengths > 0).sum())
        fixed = max(1, used // 4)
        moved = fixed + (places - fixed + offset_by * (used - fixed)) % max(1, count - fixed)
        return jnp.zeros((count,), jnp.int32).at[ranking[jnp.where(places < fixed, places, moved)]].set(jnp.asarray(lengths, jnp.int32))

    lengths = jnp.where(number % 4 == 0, named(heavy_load, number // 4), named(common, number - number // 4 - 1))
    mixed = jax.random.permutation(jax.random.fold_in(own, 3), count)
    donor, taker = mixed[0:count // 2 * 2:2], mixed[1:count // 2 * 2:2]
    room = jnp.minimum(lengths[donor] - 1, most - lengths[taker]) // 2
    room = jnp.where((donor == ranking[0]) | (taker == ranking[0]) | (lengths[taker] == 0), 0, jnp.maximum(room, 0))
    moved = jax.random.randint(jax.random.fold_in(own, 4), (count // 2,), 0, 1 << 20) % (room + 1)
    lengths = lengths.at[donor].add(-moved).at[taker].add(moved)
    items = jnp.searchsorted(jnp.cumsum(lengths), jnp.arange(rows * top), side="right").astype(jnp.int32)
    grid = items.reshape(top, rows).T
    grid = grid[jax.random.permutation(jax.random.fold_in(own, 1), rows)]
    offset_by = jax.random.randint(jax.random.fold_in(own, 2), (rows, 1), 0, top)
    return jnp.take_along_axis(grid, (jnp.arange(top)[None, :] + offset_by) % top, axis=1)


def portions_of(number_of, total, bound, slope, full):
    portions = [(1 << 20) // math.isqrt(rank ** slope) + 1 for rank in range(1, number_of + 1)]
    largest = bound if full else min(bound, max(-(-total // number_of), total * portions[0] // sum(portions)))
    least = 1 if total - largest >= number_of - 1 else 0
    counts, surplus = [largest] + [least] * (number_of - 1), total - largest - least * (number_of - 1)
    while surplus > 0:
        candidates = [i for i in range(1, number_of) if counts[i] < largest] or [i for i in range(1, number_of) if counts[i] < bound]
        mass, remaining = sum([portions[i] for i in candidates]), surplus
        for i in candidates:
            more = min(bound - counts[i], max(1, remaining * portions[i] // mass), surplus)
            counts[i] = counts[i] + more
            surplus = surplus - more
    return np.array(counts)


def centred(rng, dims, scale, bound, split=(), held_as=jnp.bfloat16):
    gain = steps_of(rng, dims, split, -0.22, 0.18) if split else 1.0
    array = jax.random.normal(rng, dims, jnp.float32) * scale * gain
    return jnp.minimum(jnp.maximum(array, -bound), bound).astype(held_as)


def setup_inputs(seed: int = 0) -> dict:
    splits = jax.random.split(jax.random.key(seed), 6)
    tokens = centred(splits[0], (TOKENS, D), 1.0, 6.0, ((0, 16),))
    route_ids_keys = jax.random.split(jax.random.fold_in(splits[1], 1), TOKENS // TOK_DEV)
    route_ids_turns = jax.random.permutation(jax.random.fold_in(splits[1], 3), TOKENS // TOK_DEV)
    route_ids = jax.vmap(lambda own, number: deal_out(jax.random.fold_in(splits[1], 2), own, number, TOK_DEV, NROUTE, TOP, CAP, 2))(route_ids_keys, route_ids_turns).reshape((TOKENS, TOP))
    whiten = centred(splits[2], (EXPERTS, D, D), D ** -0.5, 0.09375, ((0, 2), (1, 16)))
    deltas = centred(splits[3], (EXPERTS, D, H), 1.0, 6.0, ((0, 2), (1, 16)))
    basis = centred(splits[4], (D, R), D ** -0.5, 0.09375, ((0, 2),))
    return dict(tokens=tokens, route_ids=route_ids, whiten=whiten, deltas=deltas, basis=basis)


def reference(tokens, route_ids, whiten, deltas, basis):
    scale = NROUTE / (TOP * TOKENS)
    expert_ids = jnp.arange(GRAM_EXP, dtype=jnp.int32)
    hits = jnp.any(route_ids[:, :, None] == expert_ids[None, None, :], axis=1)
    hit = hits.astype(jnp.bfloat16)
    grams = []
    for index in range(GRAM_EXP):
        weighted = tokens * hit[:, index:index + 1]
        grams.append(jnp.dot(weighted.T, tokens, preferred_element_type=jnp.float32) * scale)
    gram = jnp.stack(grams, axis=1)

    def one_expert(pair):
        factor, delta = pair
        whitened = jnp.dot(factor, basis, preferred_element_type=jnp.float32).astype(jnp.bfloat16)
        return jnp.dot(whitened.T, delta, preferred_element_type=jnp.float32)

    stacked = lax.map(one_expert, (whiten, deltas))
    coefficients = jnp.transpose(stacked, (1, 0, 2))
    basis_gram = jnp.einsum("keh,leh->kl", coefficients, coefficients, precision=lax.Precision.HIGHEST) / (EXPERTS * H)
    return gram, coefficients, basis_gram
```

```python
import jax
import jax.numpy as jnp
from jax import lax
from jax.experimental import pallas as pl
from jax.experimental.pallas import tpu as pltpu
from jax.sharding import Mesh, PartitionSpec as P

NROUTE = 128
TOP = 8
GRAM_EXP = 1
CAP = 128
BF = jnp.bfloat16
F32 = jnp.float32


def factors(mesh):
    tok_count = mesh.shape["tok"]
    devices = mesh.devices.reshape(tok_count, -1)[:, 0]
    cores = 2
    spots = [tuple(d.coords) for d in devices[::cores]]
    inner = 1
    moved = [i for i in range(3) if len(spots) > 1 and spots[1][i] != spots[0][i]]
    while inner < len(spots) and all(
        spots[inner][i] == spots[0][i] for i in range(3) if i not in moved
    ):
        inner += 1
    return len(spots) // inner, inner, cores


def shift_to(x, axis, s, n):
    return lax.ppermute(x, axis, [(i, (i + s) % n) for i in range(n)])


def swap_core(x):
    return lax.ppermute(x, "c", [(0, 1), (1, 0)])


def rolled(blocks, index):
    both = jnp.stack(blocks + blocks)
    n = len(blocks)
    return lax.dynamic_slice_in_dim(both, (n - index) % n, n, 0)


def dot(a, b, dims):
    return lax.dot_general(a, b, (dims, ((), ())), preferred_element_type=F32)


def chunk_kernel(A, B, nb, cw, cores, col_offs, s_ref, w_own, w_rec, d_own, d_rec, *rest):
    basis, (send, keep, acc) = rest[:-3], rest[-3:]
    i = pl.program_id(0)
    total = None
    for w, d in ((w_own, d_own), (w_rec, d_rec)):
        wt = None
        for n, b in enumerate(basis):
            depth = b.shape[0]
            off = pl.multiple_of(s_ref[col_offs + n], depth)
            lhs = w[0, :, pl.ds(off, depth)] if len(w.shape) == 3 else w[:, pl.ds(off, depth)]
            part = dot(lhs, b[...], ((1,), (0,)))
            wt = part if wt is None else wt + part
        rhs = d[0] if len(d.shape) == 3 else d[...]
        part = dot(wt.astype(BF), rhs, ((0,), (0,)))
        total = part if total is None else total + part

    @pl.when(i == 0)
    def _():
        acc[...] = total

    @pl.when(i > 0)
    def _():
        acc[...] += total

    @pl.when(i == pl.num_programs(0) - 1)
    def _():
        width = acc.shape[0] // nb
        kb = width // B
        hb = acc.shape[1] // A
        for s in range(B):
            place = lax.rem(s_ref[1] + s, B)
            for j in range(nb):
                rows = pl.ds(pl.multiple_of(j * width + place * kb, kb), kb)
                for a in range(A):
                    tile = acc[rows, a * hb : (a + 1) * hb]
                    if s == 0:
                        keep[a, j * kb : (j + 1) * kb, :] = tile
                    else:
                        send[s - 1, a, j * kb : (j + 1) * kb, :] = tile.astype(BF)


def chunk_product(scalars, whiten, w_rec, deltas, d_rec, basis, nb, A, B, steps=2):
    _, rows, width = whiten.shape
    hidden = deltas.shape[2]
    block = rows // steps
    cols = basis[0].shape[1]
    full = lambda b: pl.BlockSpec(b.shape, lambda i, s: (0, 0))
    kernel = lambda *refs: chunk_kernel(A, B, nb, None, 2, 4, *refs)
    return pl.pallas_call(
        kernel,
        grid_spec=pltpu.PrefetchScalarGridSpec(
            num_scalar_prefetch=1,
            grid=(steps,),
            in_specs=[
                pl.BlockSpec((1, block, width), lambda i, s: (s[0], i, 0)),
                pl.BlockSpec((block, width), lambda i, s: (i, 0)),
                pl.BlockSpec((1, block, hidden), lambda i, s: (s[0], i, 0)),
                pl.BlockSpec((block, hidden), lambda i, s: (i, 0)),
            ]
            + [full(b) for b in basis],
            out_specs=[
                pl.BlockSpec((B - 1, A, cols // B, hidden // A), lambda i, s: (0, 0, 0, 0)),
                pl.BlockSpec((A, cols // B, hidden // A), lambda i, s: (0, 0, 0)),
            ],
            scratch_shapes=[pltpu.VMEM((cols, hidden), F32)],
        ),
        out_shape=[
            jax.ShapeDtypeStruct((B - 1, A, cols // B, hidden // A), BF),
            jax.ShapeDtypeStruct((A, cols // B, hidden // A), F32),
        ],
        compiler_params=pltpu.CompilerParams(vmem_limit_bytes=56 << 20),
        name="chunk_product",
    )(scalars, whiten, w_rec, deltas, d_rec, *basis)


def gram_kernel(B, dev_rows, nblocks, s_ref, *refs):
    cols, rows = refs[:nblocks], refs[nblocks : 2 * nblocks]
    row_src, (send, keep) = refs[2 * nblocks], refs[2 * nblocks + 1 :]
    del row_src


def one_gram(A, B, E, tokens, hits, scale, idx):
    z, x, c, y = idx
    tok_rows, width = tokens.shape
    col_width = width // E
    dev_rows = width // (A * B * 2)
    places = jnp.cumsum(hits.astype(jnp.int32)) - 1
    pick = (places[None, :] == jnp.arange(CAP)[:, None]) & hits[None, :]
    mine = lax.dynamic_slice_in_dim(tokens, y * col_width, col_width, 1)
    own = dot(pick.astype(BF), mine, ((1,), (0,))).astype(BF)
    if A == 4:
        p1 = lax.ppermute(own, "z", [(0, 1), (1, 0), (2, 3), (3, 2)])
        p2 = lax.ppermute(own, "z", [(1, 2), (2, 1)])
        p3 = lax.ppermute(p2, "z", [(1, 0), (2, 3)])
        p4 = lax.ppermute(p1, "z", [(1, 2), (2, 1)])
        p5 = lax.ppermute(p1, "z", [(1, 3), (2, 0)])
        groups = [own, p1, jnp.concatenate([p2 + p3, p4 + p5])]
    else:
        groups = [own] + [shift_to(own, "z", s, A) for s in range(1, A)]
    blocks = []
    for g in groups:
        blocks += [g, swap_core(g)]
    start = (z * B * 2 + c) * dev_rows
    first = start - y * col_width
    if E == 2 and col_width % (B * 2 * dev_rows) == 0:
        owner = (first >= 0) & (first < col_width)
        other = start - (1 - y) * col_width
        pairs = []
        for a in range(A):
            holder = a * B * 2 * dev_rows // col_width
            pairs.append((a * E + holder, a * E + 1 - holder))

        def rows_of(b):
            at = jnp.where(owner, first, 0)
            local = lax.dynamic_slice_in_dim(b, at, (B - 1) * 2 * dev_rows + dev_rows, 1)
            local = jnp.concatenate([local[:, i * 2 * dev_rows : i * 2 * dev_rows + dev_rows] for i in range(B)], 1)
            return jnp.where(owner, local, lax.ppermute(local, ("z", "exp"), pairs))
    else:

        def rows_of(b):
            whole = lax.all_gather(b, "exp", axis=1, tiled=True)
            return jnp.concatenate(
                [lax.dynamic_slice_in_dim(whole, start + i * 2 * dev_rows, dev_rows, 1) for i in range(B)], 1
            )

    rows = jnp.concatenate([rows_of(b) for b in blocks])
    cols = jnp.concatenate(blocks)

    def part(s):
        lhs = lax.dynamic_slice_in_dim(rows, (x + s) % B * dev_rows, dev_rows, 1)
        return dot(lhs, cols, ((0,), (0,)))

    sends = [shift_to(part(s).astype(BF), "x", s, B) for s in range(1, B)]
    total = part(0)
    for r in sends:
        total = total + r.astype(F32)
    return total * scale


def build(mesh):
    A, B, C = factors(mesh)
    E = mesh.shape["exp"]

    def shards(tokens, route_ids, whiten, deltas, basis):
        z, x, c, y = (lax.axis_index(n).astype(jnp.int32) for n in ("z", "x", "c", "exp"))
        tok_rows, width = tokens.shape
        scale = NROUTE / (TOP * tok_rows * A * B * C)
        local_experts, factor_rows, _ = whiten.shape
        hidden = deltas.shape[2]
        rank = basis.shape[1]
        half = basis.shape[0] // 2
        ka = rank // A
        sets = [list(range(0, A // 2)), list(range(A // 2, A))]

        mine = lax.dynamic_slice_in_dim(basis, c * half, half, 0)
        fetched = []
        for js in sets:
            cols = mine[:, js[0] * ka : (js[-1] + 1) * ka]
            got = [shift_to(cols, "exp", -s % E, E) for s in range(1, E)]
            fetched.append(got)
        w_rec = swap_core(lax.dynamic_index_in_dim(whiten, 1 - c, 0, False))
        d_rec = swap_core(lax.dynamic_index_in_dim(deltas, 1 - c, 0, False))
        offs = [y * 2 * half]
        for s in range(1, E):
            at = (y + s) % E * 2 * half
            offs += [at + c * half, at + (1 - c) * half]
        scalars = jnp.stack([c, x, z, y] + offs).astype(jnp.int32)

        coefs = []
        for js, got in zip(sets, fetched):
            cols = slice(js[0] * ka, (js[-1] + 1) * ka)
            parts = [basis[:, cols]]
            for g in got:
                parts += [g, swap_core(g)]
            send, keep = chunk_product(scalars, whiten, w_rec, deltas, d_rec, parts, len(js), A, B)
            got_x = [shift_to(send[s - 1], "x", s, B) for s in range(1, B)]

            def at(a):
                out = lax.dynamic_index_in_dim(keep, a, 0, False)
                for r in got_x:
                    out = out + lax.dynamic_index_in_dim(r, a, 0, False).astype(F32)
                return out

            total = at(z)
            for s in range(1, A):
                total = total + shift_to(at((z + s) % A).astype(BF), "z", s, A).astype(F32)
            coefs.append(total.reshape(len(js), ka // B, hidden // A))
        coef = jnp.concatenate(coefs)

        low = coef.astype(BF)
        blocks = [lax.dynamic_index_in_dim(coef, z, 0, False)] + [
            shift_to(lax.dynamic_index_in_dim(low, (z - s) % A, 0, False), "z", -s % A, A).astype(F32)
            for s in range(1, A)
        ]
        rows = jnp.swapaxes(rolled(blocks, z), 0, 1).reshape(C, ka // (B * C), hidden)
        own = lax.dynamic_index_in_dim(rows, c, 0, False)
        other = swap_core(lax.dynamic_index_in_dim(rows, 1 - c, 0, False))
        coefficients = jnp.where(c == 0, jnp.stack([own, other], 1), jnp.stack([other, own], 1))

        ks = rolled([low] + [shift_to(low, "x", -s % B, B) for s in range(1, B)], x)
        ks = jnp.swapaxes(ks, 0, 1).reshape(rank, hidden // A)
        prod = dot(low.reshape(rank // B, hidden // A), ks, ((1,), (1,)))
        prod = prod.reshape(A, C, ka // (B * C), rank)
        mineh = lax.dynamic_index_in_dim(prod, c, 1, False)
        mineh = mineh + swap_core(lax.dynamic_index_in_dim(prod, 1 - c, 1, False).astype(BF)).astype(F32)
        bg = lax.dynamic_index_in_dim(mineh, z, 0, False)
        for s in range(1, A):
            blk = lax.dynamic_index_in_dim(mineh, (z + s) % A, 0, False)
            bg = bg + shift_to(blk.astype(BF), "z", s, A).astype(F32)
        if E == 2:
            bg = bg.astype(BF)
            bg = bg.astype(F32) + shift_to(bg, "exp", 1, E).astype(F32)
        else:
            bg = lax.psum(bg, "exp")
        basis_gram = bg / (local_experts * E * hidden)

        grams = []
        for g in range(GRAM_EXP):
            hits = jnp.any(route_ids == g, axis=1)
            grams.append(one_gram(A, B, E, tokens, hits, scale, (z, x, c, y)))
        return jnp.stack(grams, 1), coefficients, basis_gram

    return shards, (A, B, C, E)


def solution(mesh):
    shards, (A, B, C, E) = build(mesh)
    fine = Mesh(mesh.devices.reshape(A, B, C, E), ("z", "x", "c", "exp"))
    tok = ("z", "x", "c")
    placed = (P(tok, None), P(tok, None), P("exp", tok, None), P("exp", tok, None), P("exp", None))
    return jax.shard_map(
        shards,
        mesh=fine,
        in_specs=placed,
        out_specs=(P(tok, None, "exp"), P(tok, "exp", None), P(tok, None)),
        check_vma=False,
    )
```

```python
import jax
import jax.numpy as jnp
from jax import lax
from jax.experimental import pallas as pl
from jax.experimental.pallas import tpu as pltpu
from jax.sharding import Mesh, PartitionSpec as P

NROUTE = 128
TOP = 8
GRAM_EXP = 1
CAP = 128
BF = jnp.bfloat16
F32 = jnp.float32


def factors(mesh):
    tok_count = mesh.shape["tok"]
    devices = mesh.devices.reshape(tok_count, -1)[:, 0]
    cores = 2
    spots = [tuple(d.coords) for d in devices[::cores]]
    inner = 1
    moved = [i for i in range(3) if len(spots) > 1 and spots[1][i] != spots[0][i]]
    while inner < len(spots) and all(
        spots[inner][i] == spots[0][i] for i in range(3) if i not in moved
    ):
        inner += 1
    return len(spots) // inner, inner, cores


def shift_to(x, axis, s, n):
    return lax.ppermute(x, axis, [(i, (i + s) % n) for i in range(n)])


def pairs_up(n):
    return n & (n - 1) == 0


def partner(i, m, n, back=False):
    if pairs_up(n):
        return i ^ m
    return (i - m) % n if back else (i + m) % n


def exchange(x, axis, m, n):
    return lax.ppermute(x, axis, [(i, partner(i, m, n)) for i in range(n)])


def swap_core(x):
    return lax.ppermute(x, "c", [(0, 1), (1, 0)])


def dot(a, b, dims):
    return lax.dot_general(a, b, (dims, ((), ())), preferred_element_type=F32)


PARAMS = pltpu.CompilerParams(vmem_limit_bytes=20 << 20)


def in_hbm(*arrays):
    return [pltpu.with_memory_space_constraint(a, pltpu.HBM) for a in arrays]


def whole(shape):
    return pl.BlockSpec(tuple(shape), lambda i, s: (0,) * len(shape))


def call(kernel, steps, scalars, ins, in_specs, outs, out_specs, scratch=()):
    return pl.pallas_call(
        kernel,
        grid_spec=pltpu.PrefetchScalarGridSpec(
            num_scalar_prefetch=1,
            grid=(steps,),
            in_specs=in_specs,
            out_specs=out_specs,
            scratch_shapes=list(scratch),
        ),
        out_shape=outs,
        compiler_params=PARAMS,
    )(scalars, *ins)


FETCHED = 6


def local_kernel(s_ref, w_own, w_rec, b, out):
    @pl.when(pl.program_id(0) == 0)
    def _():
        for n, w in enumerate((w_own, w_rec)):
            out[n] = dot(w[0], b[...], ((1,), (0,)))

    @pl.when(pl.program_id(0) > 0)
    def _():
        for n, w in enumerate((w_own, w_rec)):
            out[n] += dot(w[0], b[...], ((1,), (0,)))


def local_part(scalars, whiten, w_rec, basis, steps=4):
    _, rows, _ = whiten.shape
    depth, rank = basis.shape
    block = depth // steps
    spec = pl.BlockSpec((1, rows, block), lambda i, s: (s[0], 0, s[3] * steps + i))
    out = jax.ShapeDtypeStruct((2, rows, rank), F32)
    b_spec = pl.BlockSpec((block, rank), lambda i, s: (i, 0))
    return call(local_kernel, steps, scalars, in_hbm(whiten, w_rec, basis), [spec, spec, b_spec], out, whole(out.shape))


def chunk_kernel(A, B, nb, nparts, s_ref, *refs):
    ws, refs = refs[: 2 * nparts], refs[2 * nparts :]
    basis, (local, d_own, d_rec, send, keep, wt, turned, deltas, sems) = refs[:nparts], refs[nparts:]
    i = pl.program_id(0)
    copies = [pltpu.make_async_copy(d.at[s_ref[0]], deltas.at[n], sems.at[n]) for n, d in enumerate((d_own, d_rec))]

    @pl.when(i == 0)
    def _():
        for copy in copies:
            copy.start()
        wt[...] = local[...]

    for n in range(2):
        part = None
        for w, b in zip(ws[n * nparts :], basis):
            more = dot(w[0], b[...], ((1,), (0,)))
            part = more if part is None else part + more
        wt[n] += part

    @pl.when(i == pl.num_programs(0) - 1)
    def _():
        rows = wt.shape[1]
        for n in range(2):
            turned[:, n * rows : (n + 1) * rows] = wt[n].T.astype(BF)
        for copy in copies:
            copy.wait()
        width = turned.shape[0] // nb
        kb = width // B
        hb = deltas.shape[2] // A
        for s in (*range(1, B), 0):
            place = lax.rem(s_ref[1] + s, B)
            lhs = jnp.concatenate([turned[pl.ds(pl.multiple_of(j * width + place * kb, kb), kb), :] for j in range(nb)])
            part = dot(lhs[:, :rows], deltas[0], ((1,), (0,))) + dot(lhs[:, rows:], deltas[1], ((1,), (0,)))
            for a in range(A):
                tile = part[:, a * hb : (a + 1) * hb]
                if s == 0:
                    keep[a] = tile
                else:
                    send[s - 1, a] = tile.astype(BF)


def chunk_product(scalars, whiten, w_rec, deltas, d_rec, local, basis, col, nb, A, B, steps=2):
    _, rows, _ = whiten.shape
    hidden = deltas.shape[2]
    half, cols = basis[0].shape
    block = half // steps
    n = len(basis)
    factor = [
        pl.BlockSpec((1, rows, block), lambda i, s, m=m: (s[0], 0, s[FETCHED + m] * steps + i)) for m in range(n)
    ]
    outs = [(B - 1, A, cols // B, hidden // A), (A, cols // B, hidden // A)]
    return call(
        lambda *refs: chunk_kernel(A, B, nb, n, *refs),
        steps,
        scalars,
        in_hbm(*[whiten] * n, *[w_rec] * n) + list(basis) + [local] + in_hbm(deltas, d_rec),
        factor * 2
        + [pl.BlockSpec((block, cols), lambda i, s: (i, 0)) for b in basis]
        + [pl.BlockSpec((2, rows, cols), lambda i, s: (0, 0, col))]
        + [pl.BlockSpec(memory_space=pl.ANY)] * 2,
        [pltpu.HBM(outs[0], BF), pltpu.HBM(outs[1], F32)],
        [whole(o) for o in outs],
        [
            pltpu.VMEM((2, rows, cols), F32),
            pltpu.VMEM((cols, 2 * rows), BF),
            pltpu.VMEM((2, rows, hidden), BF),
            pltpu.SemaphoreType.DMA((2,)),
        ],
    )


def merge_kernel(B, span, groups, s_ref, *refs):
    ins, (out, rows) = list(refs[:-2]), refs[-2:]
    row = 0
    for size in groups:
        block = ins.pop(0)[...]
        for _ in range(size - 1):
            block = jnp.where(s_ref[4] > 0, block, ins.pop(0)[...])
        depth = block.shape[0]
        out[row : row + depth, :] = block
        row += depth
    for core in range(2):
        place = (s_ref[0] + core) % 2
        for i in range(B):
            lanes = pl.ds(pl.multiple_of(s_ref[5] + (2 * i + place) * span, span), span)
            rows[core, :, i * span : (i + 1) * span] = out[:, lanes]


def merge(scalars, groups, B, span):
    ins = [b for group in groups for b in group]
    count = sum(group[0].shape[0] for group in groups)
    outs = [(count, ins[0].shape[1]), (2, count, B * span)]
    sizes = [len(group) for group in groups]
    return call(
        lambda *refs: merge_kernel(B, span, sizes, *refs),
        1,
        scalars,
        ins,
        [whole(b.shape) for b in ins],
        [jax.ShapeDtypeStruct(o, BF) for o in outs],
        [whole(o) for o in outs],
    )


def gram_kernel(n, B, s_ref, *refs):
    cols, rows, (keep, send, turned) = refs[:n], refs[n : 2 * n], refs[2 * n :]
    span = keep.shape[0]

    @pl.when(pl.program_id(0) == 0)
    def _():
        for s in range(B):
            lanes = pl.ds(pl.multiple_of(lax.rem(s_ref[1] + s, B) * span, span), span)
            at = 0
            for r in rows:
                turned[s * span : (s + 1) * span, at : at + r.shape[0]] = r[:, lanes].T
                at += r.shape[0]

    total, at = None, 0
    for c in cols:
        part = dot(turned[:, at : at + c.shape[0]], c[...], ((1,), (0,)))
        total = part if total is None else total + part
        at += c.shape[0]
    keep[...] = total[:span]
    for s in range(1, B):
        send[s - 1] = total[s * span : (s + 1) * span].astype(BF)


def gram_part(scalars, cols, rows, piece, pieces, B, span, steps=2):
    width = cols[0].shape[1] // pieces
    tile = width // steps
    return call(
        lambda *refs: gram_kernel(len(cols), B, *refs),
        steps,
        scalars,
        list(cols) + list(rows),
        [pl.BlockSpec((c.shape[0], tile), lambda i, sc: (0, piece * steps + i)) for c in cols]
        + [whole(r.shape) for r in rows],
        [pltpu.HBM((span, width), F32), pltpu.HBM((B - 1, span, width), BF)],
        [
            pl.BlockSpec((span, tile), lambda i, sc: (0, i)),
            pl.BlockSpec((B - 1, span, tile), lambda i, sc: (0, 0, i)),
        ],
        [pltpu.VMEM((B * span, sum(r.shape[0] for r in rows)), BF)],
    )


def finish_kernel(scale, pieces, n, s_ref, *refs):
    out = refs[-1]
    tiles = sum(r.shape[1] for r in refs[:pieces]) // 128
    j = 0
    for p in range(pieces):
        total = refs[p][...]
        for r in refs[pieces + p * n : pieces + (p + 1) * n]:
            total = total + r[...].astype(F32)
        total = total * scale
        rows, width = total.shape
        for at in range(0, width, 128):
            out[pl.ds(j, rows, stride=tiles), :] = total[:, at : at + 128]
            j += 1


def finish(scalars, keeps, gots, scale, steps=4):
    rows = keeps[0].shape[0]
    block = rows // steps
    ins = list(keeps) + [g for got in gots for g in got]
    tiles = sum(k.shape[1] for k in keeps) // 128
    out = call(
        lambda *refs: finish_kernel(scale, len(keeps), len(gots[0]), *refs),
        steps,
        scalars,
        ins,
        [pl.BlockSpec((block, k.shape[1]), lambda i, s: (i, 0)) for k in ins],
        jax.ShapeDtypeStruct((rows * tiles, 128), F32),
        pl.BlockSpec((block * tiles, 128), lambda i, s: (i, 0)),
    )
    return out.reshape(rows, tiles * 128)


def product_kernel(A, B, sets, s_ref, *refs):
    n = len(sets)
    ins, (keep, away, rows, own) = refs[: B * n], refs[B * n :]
    kb = own.shape[0] // A
    for s in range(B):
        place = lax.rem(s_ref[1] + s, B)
        for m, js in enumerate(sets):
            for i, a in enumerate(js):
                block = ins[s * n + m][i]
                rows[pl.ds(pl.multiple_of((a * B + place) * kb, 16), kb), :] = block
                if s == 0:
                    own[a * kb : (a + 1) * kb, :] = block
    total = dot(own[...], rows[...], ((1,), (1,)))
    half = kb // 2
    for c in range(2):
        @pl.when(s_ref[0] == c)
        def _(c=c):
            for a in range(A):
                keep[a] = total[a * kb + c * half : a * kb + (c + 1) * half]
                away[a] = total[a * kb + (1 - c) * half : a * kb + (2 - c) * half].astype(BF)


def product(scalars, lows, others, sets, A, B):
    kb, depth = lows[0].shape[1:]
    ins = list(lows) + [o[s] for s in range(B - 1) for o in others]
    shape = (A, kb // 2, A * B * kb)
    return call(
        lambda *refs: product_kernel(A, B, sets, *refs),
        1,
        scalars,
        ins,
        [whole(k.shape) for k in ins],
        [jax.ShapeDtypeStruct(shape, F32), jax.ShapeDtypeStruct(shape, BF)],
        [whole(shape)] * 2,
        [pltpu.VMEM((A * B * kb, depth), BF), pltpu.VMEM((A * kb, depth), BF)],
    )


def rows_kernel(A, s_ref, *refs):
    ins, (mine, away) = refs[:A], refs[A:]
    kb, hb = ins[0].shape
    half = kb // 2
    for s, block in enumerate(ins):
        lanes = pl.ds(pl.multiple_of(partner(s_ref[2], s, A, True) * hb, hb), hb)
        mine[:, lanes] = block[pl.ds(pl.multiple_of(s_ref[0] * half, 8), half), :]
        away[:, lanes] = block[pl.ds(pl.multiple_of((1 - s_ref[0]) * half, 8), half), :]


def own_rows(scalars, blocks, A):
    kb, hb = blocks[0].shape
    shape = (kb // 2, A * hb)
    return call(
        lambda *refs: rows_kernel(A, *refs),
        1,
        scalars,
        blocks,
        [whole(b.shape) for b in blocks],
        [jax.ShapeDtypeStruct(shape, F32)] * 2,
        [whole(shape)] * 2,
    )


def pair_kernel(s_ref, mine, other, out):
    for c in range(2):
        @pl.when(s_ref[0] == c)
        def _(c=c):
            out[:, c, :] = mine[...]
            out[:, 1 - c, :] = other[...]


def pair(scalars, mine, other):
    shape = (mine.shape[0], 2, mine.shape[1])
    return call(
        pair_kernel, 1, scalars, [mine, other], [whole(mine.shape)] * 2, jax.ShapeDtypeStruct(shape, F32), whole(shape)
    )


def build(mesh):
    A, B, C = factors(mesh)
    E = mesh.shape["exp"]

    def shards(tokens, route_ids, whiten, deltas, basis):
        z, x, c, y = (lax.axis_index(n).astype(jnp.int32) for n in ("z", "x", "c", "exp"))
        tok_rows, width = tokens.shape
        scale = NROUTE / (TOP * tok_rows * A * B * C)
        local_experts, _, _ = whiten.shape
        hidden = deltas.shape[2]
        rank = basis.shape[1]
        half = basis.shape[0] // 2
        ka = rank // A
        col_width = width // E
        span = width // (A * B * C)
        sets = [list(range(0, A // 2)), list(range(A // 2, A))]
        spans = [slice(js[0] * ka, (js[-1] + 1) * ka) for js in sets]

        middle = ((z == 1) | (z == 2)).astype(jnp.int32)
        group_at = z * (B * C * span)
        first = group_at - y * col_width
        holder = (first >= 0) & (first + B * C * span <= col_width)
        scalars = [c, x, z, y, middle, jnp.where(holder, first, 0)]
        for s in range(1, E):
            scalars += [(y + s) % E * 2 + c, (y + s) % E * 2 + 1 - c]
        scalars = jnp.stack(scalars).astype(jnp.int32)

        w_rec = swap_core(whiten)
        d_rec = swap_core(deltas)

        def fetch(n, basis):
            cols = spans[n]
            mine = lax.dynamic_slice(basis, (c * half, cols.start), (half, cols.stop - cols.start))
            got = []
            for s in range(1, E):
                got.append(shift_to(mine, "exp", -s % E, E))
            return got

        fetched = [fetch(0, basis)]

        def routed(g):
            hits = jnp.any(route_ids == g, axis=1)
            places = jnp.cumsum(hits.astype(jnp.int32)) - 1
            pick = (places[None, :] == jnp.arange(CAP)[:, None]) & hits[None, :]
            mine = lax.dynamic_slice_in_dim(tokens, y * col_width, col_width, 1)
            own = dot(pick.astype(BF), mine, ((1,), (0,))).astype(BF)
            nonlocal later
            own, later = lax.optimization_barrier((own, basis))
            if A != 4:
                return [[[own]] + [[shift_to(own, "z", s, A)] for s in range(1, A)]]
            p1 = lax.ppermute(own, "z", [(0, 1), (1, 0), (2, 3), (3, 2)])
            p2 = lax.ppermute(own, "z", [(1, 2), (2, 1)])
            p3 = lax.ppermute(p2, "z", [(1, 0), (2, 3)])
            p4 = lax.ppermute(p1, "z", [(1, 2), (2, 1)])
            p5 = lax.ppermute(p1, "z", [(1, 3), (2, 0)])
            return [[[own], [p1]], [[p2, p3], [p4, p5]]]

        def gram_sends(groups):
            cols, rows = [], []
            for blocks in groups:
                both, part = merge(scalars, blocks, B, span)
                other = swap_core(both)
                if E == 2 and col_width % (B * C * span) == 0:
                    pairs = []
                    for a in range(A):
                        h = a * B * C * span // col_width
                        pairs.append((a * E + h, a * E + 1 - h))
                    got = lax.ppermute(part, ("z", "exp"), pairs)
                    part = jnp.where(holder, part, got)
                else:
                    every = lax.all_gather(both, "exp", axis=1, tiled=True)
                    mine = lax.dynamic_slice_in_dim(every, group_at, B * C * span, 1)
                    mine = mine.reshape(-1, B, C, span)
                    part = jnp.stack(
                        [lax.dynamic_index_in_dim(mine, (c + k) % C, 2, False).reshape(-1, B * span) for k in range(C)]
                    )
                cols += [both, other]
                rows += [part[0], swap_core(part[1])]
            keeps, gots = [], []
            for piece in range(2):
                keep, send = gram_part(scalars, cols, rows, piece, 2, B, span)
                gots.append([shift_to(send[s - 1], "x", s, B) for s in range(1, B)])
                keeps.append(keep)
            return keeps, gots

        local = local_part(scalars, whiten, w_rec, basis)

        later = basis
        routed_all = [routed(g) for g in range(GRAM_EXP)]
        fetched += [fetch(n, later) for n in range(1, len(spans))]
        grams = [gram_sends(r) for r in routed_all]

        coefs, lows, others = [], [], []
        for js, cols, got in zip(sets, spans, fetched):
            parts = []
            for g in got:
                parts += [g, swap_core(g)]
            send, keep = chunk_product(
                scalars, whiten, w_rec, deltas, d_rec, local, parts, cols.start // (cols.stop - cols.start), len(js), A, B
            )
            got_x = [shift_to(send[s - 1], "x", s, B) for s in range(1, B)]

            def at(a):
                out = lax.dynamic_index_in_dim(keep, a, 0, False)
                for r in got_x:
                    out = out + lax.dynamic_index_in_dim(r, a, 0, False).astype(F32)
                return out

            total = at(z)
            away = [at(partner(z, s, A)).astype(BF) for s in range(1, A)]
            for s in range(1, A):
                away[s - 1] = exchange(away[s - 1], "z", s, A)
            for blk in away:
                total = total + blk.astype(F32)
            coef = total.reshape(len(js), ka // B, hidden // A)
            coefs.append(coef)
            lows.append(coef.astype(BF))
            others.append([shift_to(lows[-1], "x", -s % B, B) for s in range(1, B)])
        mineh, away = product(scalars, lows, others, sets, A, B)
        away = swap_core(away)
        mineh = mineh + away.astype(F32)
        bg = lax.dynamic_index_in_dim(mineh, z, 0, False)
        for s in range(1, A):
            blk = lax.dynamic_index_in_dim(mineh, partner(z, s, A), 0, False).astype(BF)
            blk = exchange(blk, "z", s, A)
            bg = bg + blk.astype(F32)
        if E == 2:
            bg = bg.astype(BF)
            got = shift_to(bg, "exp", 1, E)
            bg = bg.astype(F32) + got.astype(F32)
        else:
            bg = lax.psum(bg, "exp")
        basis_gram = bg / (local_experts * E * hidden)

        coef = jnp.concatenate(coefs)
        blocks = [lax.dynamic_index_in_dim(coef, z, 0, False)]
        for s in range(1, A):
            blk = lax.dynamic_index_in_dim(coef, partner(z, s, A), 0, False)
            blocks.append(exchange(blk, "z", s, A))
        mine, other = own_rows(scalars, blocks, A)
        other = swap_core(other)
        coefficients = pair(scalars, mine, other)

        out = [finish(scalars, keeps, gots, scale) for keeps, gots in grams]
        return jnp.stack(out, 1), coefficients, basis_gram

    def named(*args):
        return shards(*args)

    return named, (A, B, C, E)


def solution(mesh):
    shards, (A, B, C, E) = build(mesh)
    fine = Mesh(mesh.devices.reshape(A, B, C, E), ("z", "x", "c", "exp"))
    tok = ("z", "x", "c")
    placed = (P(tok, None), P(tok, None), P("exp", tok, None), P("exp", tok, None), P("exp", None))
    return jax.shard_map(
        shards,
        mesh=fine,
        in_specs=placed,
        out_specs=(P(tok, None, "exp"), P(tok, "exp", None), P(tok, None)),
        check_vma=False,
    )
```

```python
import jax
import jax.numpy as jnp
from jax import lax
from jax.experimental import pallas as pl
from jax.experimental.pallas import tpu as pltpu
from jax.sharding import Mesh, PartitionSpec as P

NROUTE = 128
TOP = 8
GRAM_EXP = 1
CAP = 128
BF = jnp.bfloat16
F32 = jnp.float32


def factors(mesh):
    tok_count = mesh.shape["tok"]
    devices = mesh.devices.reshape(tok_count, -1)[:, 0]
    cores = 2
    spots = [tuple(d.coords) for d in devices[::cores]]
    inner = 1
    moved = [i for i in range(3) if len(spots) > 1 and spots[1][i] != spots[0][i]]
    while inner < len(spots) and all(
        spots[inner][i] == spots[0][i] for i in range(3) if i not in moved
    ):
        inner += 1
    return len(spots) // inner, inner, cores


def shift_to(x, axis, s, n):
    return lax.ppermute(x, axis, [(i, (i + s) % n) for i in range(n)])


def pairs_up(n):
    return n & (n - 1) == 0


def partner(i, m, n, back=False):
    if pairs_up(n):
        return i ^ m
    return (i - m) % n if back else (i + m) % n


def exchange(x, axis, m, n):
    return lax.ppermute(x, axis, [(i, partner(i, m, n)) for i in range(n)])


def swap_core(x):
    return lax.ppermute(x, "c", [(0, 1), (1, 0)])


def dot(a, b, dims):
    return lax.dot_general(a, b, (dims, ((), ())), preferred_element_type=F32)


PARAMS = pltpu.CompilerParams(vmem_limit_bytes=20 << 20)


def in_hbm(*arrays):
    return [pltpu.with_memory_space_constraint(a, pltpu.HBM) for a in arrays]


def whole(shape):
    return pl.BlockSpec(tuple(shape), lambda i, s: (0,) * len(shape))


def call(kernel, steps, scalars, ins, in_specs, outs, out_specs, scratch=()):
    return pl.pallas_call(
        kernel,
        grid_spec=pltpu.PrefetchScalarGridSpec(
            num_scalar_prefetch=1,
            grid=(steps,),
            in_specs=in_specs,
            out_specs=out_specs,
            scratch_shapes=list(scratch),
        ),
        out_shape=outs,
        compiler_params=PARAMS,
    )(scalars, *ins)


FETCHED = 5


def local_kernel(s_ref, w_own, w_rec, b, out):
    @pl.when(pl.program_id(0) == 0)
    def _():
        for n, w in enumerate((w_own, w_rec)):
            out[n] = dot(w[0], b[...], ((1,), (0,)))

    @pl.when(pl.program_id(0) > 0)
    def _():
        for n, w in enumerate((w_own, w_rec)):
            out[n] += dot(w[0], b[...], ((1,), (0,)))


def local_part(scalars, whiten, w_rec, basis, steps=4):
    _, rows, _ = whiten.shape
    depth, rank = basis.shape
    block = depth // steps
    spec = pl.BlockSpec((1, rows, block), lambda i, s: (s[0], 0, s[3] * steps + i))
    out = jax.ShapeDtypeStruct((2, rows, rank), F32)
    b_spec = pl.BlockSpec((block, rank), lambda i, s: (i, 0))
    return call(local_kernel, steps, scalars, in_hbm(whiten, w_rec, basis), [spec, spec, b_spec], out, whole(out.shape))


def chunk_kernel(A, B, nb, nparts, s_ref, *refs):
    ws, refs = refs[: 2 * nparts], refs[2 * nparts :]
    basis, (local, d_own, d_rec, send, keep, wt, turned, deltas, sems) = refs[:nparts], refs[nparts:]
    i = pl.program_id(0)
    copies = [pltpu.make_async_copy(d.at[s_ref[0]], deltas.at[n], sems.at[n]) for n, d in enumerate((d_own, d_rec))]

    @pl.when(i == 0)
    def _():
        for copy in copies:
            copy.start()
        wt[...] = local[...]

    for n in range(2):
        part = None
        for w, b in zip(ws[n * nparts :], basis):
            more = dot(w[0], b[...], ((1,), (0,)))
            part = more if part is None else part + more
        wt[n] += part

    @pl.when(i == pl.num_programs(0) - 1)
    def _():
        rows = wt.shape[1]
        for n in range(2):
            turned[:, n * rows : (n + 1) * rows] = wt[n].T.astype(BF)
        for copy in copies:
            copy.wait()
        width = turned.shape[0] // nb
        kb = width // B
        hb = deltas.shape[2] // A
        for s in (*range(1, B), 0):
            place = lax.rem(s_ref[1] + s, B)
            lhs = jnp.concatenate([turned[pl.ds(pl.multiple_of(j * width + place * kb, kb), kb), :] for j in range(nb)])
            part = dot(lhs[:, :rows], deltas[0], ((1,), (0,))) + dot(lhs[:, rows:], deltas[1], ((1,), (0,)))
            for a in range(A):
                tile = part[:, a * hb : (a + 1) * hb]
                if s == 0:
                    keep[a] = tile
                else:
                    send[s - 1, a] = tile.astype(BF)


def chunk_product(scalars, whiten, w_rec, deltas, d_rec, local, basis, col, nb, A, B, steps=2):
    _, rows, _ = whiten.shape
    hidden = deltas.shape[2]
    half, cols = basis[0].shape
    block = half // steps
    n = len(basis)
    factor = [
        pl.BlockSpec((1, rows, block), lambda i, s, m=m: (s[0], 0, s[FETCHED + m] * steps + i)) for m in range(n)
    ]
    outs = [(B - 1, A, cols // B, hidden // A), (A, cols // B, hidden // A)]
    return call(
        lambda *refs: chunk_kernel(A, B, nb, n, *refs),
        steps,
        scalars,
        in_hbm(*[whiten] * n, *[w_rec] * n) + list(basis) + [local] + in_hbm(deltas, d_rec),
        factor * 2
        + [pl.BlockSpec((block, cols), lambda i, s: (i, 0)) for b in basis]
        + [pl.BlockSpec((2, rows, cols), lambda i, s: (0, 0, col))]
        + [pl.BlockSpec(memory_space=pl.ANY)] * 2,
        [pltpu.HBM(outs[0], BF), pltpu.HBM(outs[1], F32)],
        [whole(o) for o in outs],
        [
            pltpu.VMEM((2, rows, cols), F32),
            pltpu.VMEM((cols, 2 * rows), BF),
            pltpu.VMEM((2, rows, hidden), BF),
            pltpu.SemaphoreType.DMA((2,)),
        ],
    )


def merge_kernel(B, span, s_ref, *refs):
    ins, (out, rows) = refs[:-2], refs[-2:]
    at = 0
    for block in ins:
        out[at : at + block.shape[0], :] = block[...]
        for core in range(2):
            place = (s_ref[0] + core) % 2
            for i in range(B):
                lanes = pl.ds(pl.multiple_of(s_ref[4] + (2 * i + place) * span, span), span)
                rows[core, i * span : (i + 1) * span, at : at + block.shape[0]] = block[:, lanes].T
        at += block.shape[0]


def merge(scalars, blocks, B, span):
    count = sum(b.shape[0] for b in blocks)
    outs = [(count, blocks[0].shape[1]), (2, B * span, count)]
    return call(
        lambda *refs: merge_kernel(B, span, *refs),
        1,
        scalars,
        blocks,
        [whole(b.shape) for b in blocks],
        [jax.ShapeDtypeStruct(o, BF) for o in outs],
        [whole(o) for o in outs],
    )


def gram_kernel(n, B, s_ref, *refs):
    cols, rows, (keep, send) = refs[:n], refs[n : 2 * n], refs[2 * n :]
    span = keep.shape[0]
    total = None
    for c, r in zip(cols, rows):
        part = dot(r[...], c[...], ((1,), (0,)))
        total = part if total is None else total + part
    for x in range(B):

        @pl.when(s_ref[1] == x)
        def _(x=x):
            for s in range(B):
                at = (x + s) % B * span
                if s == 0:
                    keep[...] = total[at : at + span]
                else:
                    send[s - 1] = total[at : at + span].astype(BF)


def gram_part(scalars, cols, rows, first, steps, tile, B, span):
    width = steps * tile
    return call(
        lambda *refs: gram_kernel(len(cols), B, *refs),
        steps,
        scalars,
        list(cols) + list(rows),
        [pl.BlockSpec((c.shape[0], tile), lambda i, sc: (0, first + i)) for c in cols]
        + [whole(r.shape) for r in rows],
        [pltpu.HBM((span, width), F32), pltpu.HBM((B - 1, span, width), BF)],
        [
            pl.BlockSpec((span, tile), lambda i, sc: (0, i)),
            pl.BlockSpec((B - 1, span, tile), lambda i, sc: (0, 0, i)),
        ],
    )


def finish_kernel(scale, pieces, n, s_ref, *refs):
    out = refs[-1]
    tiles = sum(r.shape[1] for r in refs[:pieces]) // 128
    j = 0
    for p in range(pieces):
        total = refs[p][...]
        for r in refs[pieces + p * n : pieces + (p + 1) * n]:
            total = total + r[...].astype(F32)
        total = total * scale
        rows, width = total.shape
        for at in range(0, width, 128):
            out[pl.ds(j, rows, stride=tiles), :] = total[:, at : at + 128]
            j += 1


def finish(scalars, keeps, gots, scale, steps=4):
    rows = keeps[0].shape[0]
    block = rows // steps
    ins = list(keeps) + [g for got in gots for g in got]
    tiles = sum(k.shape[1] for k in keeps) // 128
    out = call(
        lambda *refs: finish_kernel(scale, len(keeps), len(gots[0]), *refs),
        steps,
        scalars,
        ins,
        [pl.BlockSpec((block, k.shape[1]), lambda i, s: (i, 0)) for k in ins],
        jax.ShapeDtypeStruct((rows * tiles, 128), F32),
        pl.BlockSpec((block * tiles, 128), lambda i, s: (i, 0)),
    )
    return out.reshape(rows, tiles * 128)


def product_kernel(A, B, sets, s_ref, *refs):
    n = len(sets)
    ins, (keep, away, rows, own) = refs[: B * n], refs[B * n :]
    kb = own.shape[0] // A
    for s in range(B):
        place = lax.rem(s_ref[1] + s, B)
        for m, js in enumerate(sets):
            for i, a in enumerate(js):
                block = ins[s * n + m][i]
                rows[pl.ds(pl.multiple_of((a * B + place) * kb, 16), kb), :] = block
                if s == 0:
                    own[a * kb : (a + 1) * kb, :] = block
    total = dot(own[...], rows[...], ((1,), (1,)))
    half = kb // 2
    for c in range(2):
        @pl.when(s_ref[0] == c)
        def _(c=c):
            for a in range(A):
                keep[a] = total[a * kb + c * half : a * kb + (c + 1) * half]
                away[a] = total[a * kb + (1 - c) * half : a * kb + (2 - c) * half].astype(BF)


def product(scalars, lows, others, sets, A, B):
    kb, depth = lows[0].shape[1:]
    ins = list(lows) + [o[s] for s in range(B - 1) for o in others]
    shape = (A, kb // 2, A * B * kb)
    return call(
        lambda *refs: product_kernel(A, B, sets, *refs),
        1,
        scalars,
        ins,
        [whole(k.shape) for k in ins],
        [jax.ShapeDtypeStruct(shape, F32), jax.ShapeDtypeStruct(shape, BF)],
        [whole(shape)] * 2,
        [pltpu.VMEM((A * B * kb, depth), BF), pltpu.VMEM((A * kb, depth), BF)],
    )


def rows_kernel(A, s_ref, *refs):
    ins, (mine, away) = refs[:A], refs[A:]
    kb, hb = ins[0].shape
    half = kb // 2
    for s, block in enumerate(ins):
        lanes = pl.ds(pl.multiple_of(partner(s_ref[2], s, A, True) * hb, hb), hb)
        mine[:, lanes] = block[pl.ds(pl.multiple_of(s_ref[0] * half, 8), half), :].astype(F32)
        away[:, lanes] = block[pl.ds(pl.multiple_of((1 - s_ref[0]) * half, 8), half), :].astype(F32)


def own_rows(scalars, blocks, A):
    kb, hb = blocks[0].shape
    shape = (kb // 2, A * hb)
    return call(
        lambda *refs: rows_kernel(A, *refs),
        1,
        scalars,
        blocks,
        [whole(b.shape) for b in blocks],
        [jax.ShapeDtypeStruct(shape, F32)] * 2,
        [whole(shape)] * 2,
    )


def pair_kernel(s_ref, mine, other, out):
    for c in range(2):
        @pl.when(s_ref[0] == c)
        def _(c=c):
            out[:, c, :] = mine[...]
            out[:, 1 - c, :] = other[...]


def pair(scalars, mine, other):
    shape = (mine.shape[0], 2, mine.shape[1])
    return call(
        pair_kernel, 1, scalars, [mine, other], [whole(mine.shape)] * 2, jax.ShapeDtypeStruct(shape, F32), whole(shape)
    )


TILES = 4
PIECES = ((0, 1), (1, 3))


def build(mesh):
    A, B, C = factors(mesh)
    E = mesh.shape["exp"]

    def shards(tokens, route_ids, whiten, deltas, basis):
        z, x, c, y = (lax.axis_index(n).astype(jnp.int32) for n in ("z", "x", "c", "exp"))
        tok_rows, width = tokens.shape
        scale = NROUTE / (TOP * tok_rows * A * B * C)
        local_experts, _, _ = whiten.shape
        hidden = deltas.shape[2]
        rank = basis.shape[1]
        half = basis.shape[0] // 2
        ka = rank // A
        col_width = width // E
        span = width // (A * B * C)
        sets = [list(range(0, A // 2)), list(range(A // 2, A))]
        spans = [slice(js[0] * ka, (js[-1] + 1) * ka) for js in sets]

        group_at = z * (B * C * span)
        first = group_at - y * col_width
        holder = (first >= 0) & (first + B * C * span <= col_width)
        scalars = [c, x, z, y, jnp.where(holder, first, 0)]
        for s in range(1, E):
            scalars += [(y + s) % E * 2 + c, (y + s) % E * 2 + 1 - c]
        scalars = jnp.stack(scalars).astype(jnp.int32)

        w_rec = swap_core(whiten)
        d_rec = swap_core(deltas)

        def fetch(n, basis):
            cols = spans[n]
            mine = lax.dynamic_slice(basis, (c * half, cols.start), (half, cols.stop - cols.start))
            got = []
            for s in range(1, E):
                got.append(shift_to(mine, "exp", -s % E, E))
            return got

        fetched = [fetch(0, basis)]

        last_steps = [A // 2] if A > 2 else []
        first_steps = [m for m in reversed(range(1, A)) if m not in last_steps]

        def routed(g):
            hits = jnp.any(route_ids == g, axis=1)
            places = jnp.cumsum(hits.astype(jnp.int32)) - 1
            pick = (places[None, :] == jnp.arange(CAP)[:, None]) & hits[None, :]
            mine = lax.dynamic_slice_in_dim(tokens, y * col_width, col_width, 1)
            own = dot(pick.astype(BF), mine, ((1,), (0,))).astype(BF)
            nonlocal later
            own, later = lax.optimization_barrier((own, basis))
            early = [own]
            for m in first_steps:
                early.append(exchange(own, "z", m, A))
            late = []
            for m in last_steps:
                late.append(exchange(own, "z", m, A))
            return [early, late] if late else [early]

        def gram_sends(groups):
            cols, rows = [], []
            for blocks in groups:
                both, part = merge(scalars, blocks, B, span)
                other = swap_core(both)
                if E == 2 and col_width % (B * C * span) == 0:
                    pairs = []
                    for a in range(A):
                        h = a * B * C * span // col_width
                        pairs.append((a * E + h, a * E + 1 - h))
                    got = lax.ppermute(part, ("z", "exp"), pairs)
                    part = jnp.where(holder, part, got)
                else:
                    every = lax.all_gather(both, "exp", axis=1, tiled=True)
                    mine = lax.dynamic_slice_in_dim(every, group_at, B * C * span, 1)
                    mine = mine.reshape(-1, B, C, span)
                    part = jnp.stack(
                        [lax.dynamic_index_in_dim(mine, (c + k) % C, 2, False).reshape(-1, B * span).T for k in range(C)]
                    )
                cols += [both, other]
                rows += [part[0], swap_core(part[1])]
            keeps, gots = [], []
            for first, steps in PIECES:
                keep, send = gram_part(scalars, cols, rows, first, steps, col_width // TILES, B, span)
                gots.append([shift_to(send[s - 1], "x", s, B) for s in range(1, B)])
                keeps.append(keep)
            return keeps, gots

        local = local_part(scalars, whiten, w_rec, basis)

        later = basis
        routed_all = [routed(g) for g in range(GRAM_EXP)]
        fetched += [fetch(n, later) for n in range(1, len(spans))]
        grams = [gram_sends(r) for r in routed_all]

        coefs, lows, others = [], [], []
        for js, cols, got in zip(sets, spans, fetched):
            parts = []
            for g in got:
                parts += [g, swap_core(g)]
            send, keep = chunk_product(
                scalars, whiten, w_rec, deltas, d_rec, local, parts, cols.start // (cols.stop - cols.start), len(js), A, B
            )
            got_x = [shift_to(send[s - 1], "x", s, B) for s in range(1, B)]

            def at(a):
                out = lax.dynamic_index_in_dim(keep, a, 0, False)
                for r in got_x:
                    out = out + lax.dynamic_index_in_dim(r, a, 0, False).astype(F32)
                return out

            total = at(z)
            away = [at(partner(z, s, A)).astype(BF) for s in range(1, A)]
            for s in range(1, A):
                away[s - 1] = exchange(away[s - 1], "z", s, A)
            for blk in away:
                total = total + blk.astype(F32)
            coef = total.reshape(len(js), ka // B, hidden // A)
            coefs.append(coef)
            lows.append(coef.astype(BF))
            others.append([shift_to(lows[-1], "x", -s % B, B) for s in range(1, B)])
        mineh, away = product(scalars, lows, others, sets, A, B)
        away = swap_core(away)
        mineh = mineh + away.astype(F32)
        bg = lax.dynamic_index_in_dim(mineh, z, 0, False)
        for s in range(1, A):
            blk = lax.dynamic_index_in_dim(mineh, partner(z, s, A), 0, False).astype(BF)
            blk = exchange(blk, "z", s, A)
            bg = bg + blk.astype(F32)
        if E == 2:
            bg = bg.astype(BF)
            got = shift_to(bg, "exp", 1, E)
            bg = bg.astype(F32) + got.astype(F32)
        else:
            bg = lax.psum(bg, "exp")
        basis_gram = bg / (local_experts * E * hidden)

        coef = jnp.concatenate(coefs)
        blocks = [lax.dynamic_index_in_dim(coef, z, 0, False)]
        for s in range(1, A):
            blk = lax.dynamic_index_in_dim(coef, partner(z, s, A), 0, False).astype(BF)
            blocks.append(exchange(blk, "z", s, A))
        mine, other = own_rows(scalars, blocks, A)
        other = swap_core(other)
        coefficients = pair(scalars, mine, other)

        out = [finish(scalars, keeps, gots, scale) for keeps, gots in grams]
        return jnp.stack(out, 1), coefficients, basis_gram

    def named(*args):
        return shards(*args)

    return named, (A, B, C, E)


def solution(mesh):
    shards, (A, B, C, E) = build(mesh)
    fine = Mesh(mesh.devices.reshape(A, B, C, E), ("z", "x", "c", "exp"))
    tok = ("z", "x", "c")
    placed = (P(tok, None), P(tok, None), P("exp", tok, None), P("exp", tok, None), P("exp", None))
    return jax.shard_map(
        shards,
        mesh=fine,
        in_specs=placed,
        out_specs=(P(tok, None, "exp"), P(tok, "exp", None), P(tok, None)),
        check_vma=False,
    )
```

```python
import jax
import jax.numpy as jnp
from jax import lax
from jax.experimental import pallas as pl
from jax.experimental.pallas import tpu as pltpu
from jax.sharding import Mesh, PartitionSpec as P

NROUTE = 128
TOP = 8
GRAM_EXP = 1
CAP = 128
BF = jnp.bfloat16
F32 = jnp.float32


def factors(mesh):
    tok_count = mesh.shape["tok"]
    devices = mesh.devices.reshape(tok_count, -1)[:, 0]
    cores = 2
    spots = [tuple(d.coords) for d in devices[::cores]]
    inner = 1
    moved = [i for i in range(3) if len(spots) > 1 and spots[1][i] != spots[0][i]]
    while inner < len(spots) and all(
        spots[inner][i] == spots[0][i] for i in range(3) if i not in moved
    ):
        inner += 1
    return len(spots) // inner, inner, cores


def shift_to(x, axis, s, n):
    return lax.ppermute(x, axis, [(i, (i + s) % n) for i in range(n)])


def pairs_up(n):
    return n & (n - 1) == 0


def partner(i, m, n, back=False):
    if pairs_up(n):
        return i ^ m
    return (i - m) % n if back else (i + m) % n


def exchange(x, axis, m, n):
    return lax.ppermute(x, axis, [(i, partner(i, m, n)) for i in range(n)])


def swap_core(x):
    return lax.ppermute(x, "c", [(0, 1), (1, 0)])


def dot(a, b, dims):
    return lax.dot_general(a, b, (dims, ((), ())), preferred_element_type=F32)


PARAMS = pltpu.CompilerParams(vmem_limit_bytes=20 << 20)


def in_hbm(*arrays):
    return [pltpu.with_memory_space_constraint(a, pltpu.HBM) for a in arrays]


def whole(shape):
    return pl.BlockSpec(tuple(shape), lambda i, s: (0,) * len(shape))


def call(kernel, steps, scalars, ins, in_specs, outs, out_specs, scratch=()):
    return pl.pallas_call(
        kernel,
        grid_spec=pltpu.PrefetchScalarGridSpec(
            num_scalar_prefetch=1,
            grid=(steps,),
            in_specs=in_specs,
            out_specs=out_specs,
            scratch_shapes=list(scratch),
        ),
        out_shape=outs,
        compiler_params=PARAMS,
    )(scalars, *ins)


FETCHED = 5


def local_kernel(s_ref, w_own, w_rec, b, out):
    @pl.when(pl.program_id(0) == 0)
    def _():
        for n, w in enumerate((w_own, w_rec)):
            out[n] = dot(w[0], b[...], ((1,), (0,)))

    @pl.when(pl.program_id(0) > 0)
    def _():
        for n, w in enumerate((w_own, w_rec)):
            out[n] += dot(w[0], b[...], ((1,), (0,)))


def local_part(scalars, whiten, w_rec, basis, steps=4):
    _, rows, _ = whiten.shape
    depth, rank = basis.shape
    block = depth // steps
    spec = pl.BlockSpec((1, rows, block), lambda i, s: (s[0], 0, s[3] * steps + i))
    out = jax.ShapeDtypeStruct((2, rows, rank), F32)
    b_spec = pl.BlockSpec((block, rank), lambda i, s: (i, 0))
    return call(local_kernel, steps, scalars, in_hbm(whiten, w_rec, basis), [spec, spec, b_spec], out, whole(out.shape))


def chunk_kernel(A, B, nb, nparts, s_ref, *refs):
    ws, refs = refs[: 2 * nparts], refs[2 * nparts :]
    basis, (local, d_own, d_rec, send, keep, wt, turned, deltas, sems) = refs[:nparts], refs[nparts:]
    i = pl.program_id(0)
    copies = [pltpu.make_async_copy(d.at[s_ref[0]], deltas.at[n], sems.at[n]) for n, d in enumerate((d_own, d_rec))]

    @pl.when(i == 0)
    def _():
        for copy in copies:
            copy.start()
        wt[...] = local[...]

    for n in range(2):
        part = None
        for w, b in zip(ws[n * nparts :], basis):
            more = dot(w[0], b[...], ((1,), (0,)))
            part = more if part is None else part + more
        wt[n] += part

    @pl.when(i == pl.num_programs(0) - 1)
    def _():
        rows = wt.shape[1]
        for n in range(2):
            turned[:, n * rows : (n + 1) * rows] = wt[n].T.astype(BF)
        for copy in copies:
            copy.wait()
        width = turned.shape[0] // nb
        kb = width // B
        hb = deltas.shape[2] // A
        for s in (*range(1, B), 0):
            place = lax.rem(s_ref[1] + s, B)
            lhs = jnp.concatenate([turned[pl.ds(pl.multiple_of(j * width + place * kb, kb), kb), :] for j in range(nb)])
            part = dot(lhs[:, :rows], deltas[0], ((1,), (0,))) + dot(lhs[:, rows:], deltas[1], ((1,), (0,)))
            for a in range(A):
                tile = part[:, a * hb : (a + 1) * hb]
                if s == 0:
                    keep[a] = tile
                else:
                    send[s - 1, a] = tile.astype(BF)


def chunk_product(scalars, whiten, w_rec, deltas, d_rec, local, basis, col, nb, A, B, steps=2):
    _, rows, _ = whiten.shape
    hidden = deltas.shape[2]
    half, cols = basis[0].shape
    block = half // steps
    n = len(basis)
    factor = [
        pl.BlockSpec((1, rows, block), lambda i, s, m=m: (s[0], 0, s[FETCHED + m] * steps + i)) for m in range(n)
    ]
    outs = [(B - 1, A, cols // B, hidden // A), (A, cols // B, hidden // A)]
    return call(
        lambda *refs: chunk_kernel(A, B, nb, n, *refs),
        steps,
        scalars,
        in_hbm(*[whiten] * n, *[w_rec] * n) + list(basis) + [local] + in_hbm(deltas, d_rec),
        factor * 2
        + [pl.BlockSpec((block, cols), lambda i, s: (i, 0)) for b in basis]
        + [pl.BlockSpec((2, rows, cols), lambda i, s: (0, 0, col))]
        + [pl.BlockSpec(memory_space=pl.ANY)] * 2,
        [pltpu.HBM(outs[0], BF), pltpu.HBM(outs[1], F32)],
        [whole(o) for o in outs],
        [
            pltpu.VMEM((2, rows, cols), F32),
            pltpu.VMEM((cols, 2 * rows), BF),
            pltpu.VMEM((2, rows, hidden), BF),
            pltpu.SemaphoreType.DMA((2,)),
        ],
    )


def merge_kernel(B, span, skip, s_ref, *refs):
    ins, (out, rows) = refs[:-2], refs[-2:]
    at = 0
    first = sum(block.shape[0] for block in ins[:skip])
    for n, block in enumerate(ins):
        out[at : at + block.shape[0], :] = block[...]
        at += block.shape[0]
        if n < skip:
            continue
        to = at - block.shape[0] - first
        for core in range(2):
            place = (s_ref[0] + core) % 2
            for i in range(B):
                lanes = pl.ds(pl.multiple_of(s_ref[4] + (2 * i + place) * span, span), span)
                rows[core, i * span : (i + 1) * span, to : to + block.shape[0]] = block[:, lanes].T


def merge(scalars, blocks, B, span, skip):
    count = sum(b.shape[0] for b in blocks)
    outs = [(count, blocks[0].shape[1]), (2, B * span, sum(b.shape[0] for b in blocks[skip:]))]
    return call(
        lambda *refs: merge_kernel(B, span, skip, *refs),
        1,
        scalars,
        blocks,
        [whole(b.shape) for b in blocks],
        [jax.ShapeDtypeStruct(o, BF) for o in outs],
        [whole(o) for o in outs],
    )


def gram_kernel(spots, B, s_ref, *refs):
    n = len(refs) - 2 - len(spots)
    cols, rows, (keep, send) = refs[:n], refs[n:-2], refs[-2:]
    span = keep.shape[0]
    total = None
    for (i, at), r in zip(spots, rows):
        part = dot(r[...], cols[i][at : at + r.shape[1], :], ((1,), (0,)))
        total = part if total is None else total + part
    for x in range(B):

        @pl.when(s_ref[1] == x)
        def _(x=x):
            for s in range(B):
                at = (x + s) % B * span
                if s == 0:
                    keep[...] = total[at : at + span]
                else:
                    send[s - 1] = total[at : at + span].astype(BF)


def gram_part(scalars, cols, rows, spots, first, steps, tile, B, span):
    width = steps * tile
    return call(
        lambda *refs: gram_kernel(spots, B, *refs),
        steps,
        scalars,
        list(cols) + list(rows),
        [pl.BlockSpec((c.shape[0], tile), lambda i, sc: (0, first + i)) for c in cols]
        + [whole(r.shape) for r in rows],
        [pltpu.HBM((span, width), F32), pltpu.HBM((B - 1, span, width), BF)],
        [
            pl.BlockSpec((span, tile), lambda i, sc: (0, i)),
            pl.BlockSpec((B - 1, span, tile), lambda i, sc: (0, 0, i)),
        ],
    )


def finish_kernel(scale, pieces, n, s_ref, *refs):
    out = refs[-1]
    tiles = sum(r.shape[1] for r in refs[:pieces]) // 128
    j = 0
    for p in range(pieces):
        total = refs[p][...]
        for r in refs[pieces + p * n : pieces + (p + 1) * n]:
            total = total + r[...].astype(F32)
        total = total * scale
        rows, width = total.shape
        for at in range(0, width, 128):
            out[pl.ds(j, rows, stride=tiles), :] = total[:, at : at + 128]
            j += 1


def finish(scalars, keeps, gots, scale, steps=4):
    rows = keeps[0].shape[0]
    block = rows // steps
    ins = list(keeps) + [g for got in gots for g in got]
    tiles = sum(k.shape[1] for k in keeps) // 128
    out = call(
        lambda *refs: finish_kernel(scale, len(keeps), len(gots[0]), *refs),
        steps,
        scalars,
        ins,
        [pl.BlockSpec((block, k.shape[1]), lambda i, s: (i, 0)) for k in ins],
        jax.ShapeDtypeStruct((rows * tiles, 128), F32),
        pl.BlockSpec((block * tiles, 128), lambda i, s: (i, 0)),
    )
    return out.reshape(rows, tiles * 128)


def product_kernel(A, B, sets, s_ref, *refs):
    n = len(sets)
    ins, (keep, away, rows, own) = refs[: B * n], refs[B * n :]
    kb = own.shape[0] // A
    for s in range(B):
        place = lax.rem(s_ref[1] + s, B)
        for m, js in enumerate(sets):
            for i, a in enumerate(js):
                block = ins[s * n + m][i]
                rows[pl.ds(pl.multiple_of((a * B + place) * kb, 16), kb), :] = block
                if s == 0:
                    own[a * kb : (a + 1) * kb, :] = block
    total = dot(own[...], rows[...], ((1,), (1,)))
    half = kb // 2
    for c in range(2):
        @pl.when(s_ref[0] == c)
        def _(c=c):
            for a in range(A):
                keep[a] = total[a * kb + c * half : a * kb + (c + 1) * half]
                away[a] = total[a * kb + (1 - c) * half : a * kb + (2 - c) * half].astype(BF)


def product(scalars, lows, others, sets, A, B):
    kb, depth = lows[0].shape[1:]
    ins = list(lows) + [o[s] for s in range(B - 1) for o in others]
    shape = (A, kb // 2, A * B * kb)
    return call(
        lambda *refs: product_kernel(A, B, sets, *refs),
        1,
        scalars,
        ins,
        [whole(k.shape) for k in ins],
        [jax.ShapeDtypeStruct(shape, F32), jax.ShapeDtypeStruct(shape, BF)],
        [whole(shape)] * 2,
        [pltpu.VMEM((A * B * kb, depth), BF), pltpu.VMEM((A * kb, depth), BF)],
    )


def rows_kernel(A, s_ref, *refs):
    ins, (mine, away) = refs[:A], refs[A:]
    kb, hb = ins[0].shape
    half = kb // 2
    for s, block in enumerate(ins):
        lanes = pl.ds(pl.multiple_of(partner(s_ref[2], s, A, True) * hb, hb), hb)
        mine[:, lanes] = block[pl.ds(pl.multiple_of(s_ref[0] * half, 8), half), :].astype(F32)
        away[:, lanes] = block[pl.ds(pl.multiple_of((1 - s_ref[0]) * half, 8), half), :].astype(F32)


def own_rows(scalars, blocks, A):
    kb, hb = blocks[0].shape
    shape = (kb // 2, A * hb)
    return call(
        lambda *refs: rows_kernel(A, *refs),
        1,
        scalars,
        blocks,
        [whole(b.shape) for b in blocks],
        [jax.ShapeDtypeStruct(shape, F32)] * 2,
        [whole(shape)] * 2,
    )


def pair_kernel(s_ref, mine, other, out):
    for c in range(2):
        @pl.when(s_ref[0] == c)
        def _(c=c):
            out[:, c, :] = mine[...]
            out[:, 1 - c, :] = other[...]


def pair(scalars, mine, other):
    shape = (mine.shape[0], 2, mine.shape[1])
    return call(
        pair_kernel, 1, scalars, [mine, other], [whole(mine.shape)] * 2, jax.ShapeDtypeStruct(shape, F32), whole(shape)
    )


TILES = 4
PIECES = ((0, 1), (1, 3))


def build(mesh):
    A, B, C = factors(mesh)
    E = mesh.shape["exp"]

    def shards(tokens, route_ids, whiten, deltas, basis):
        z, x, c, y = (lax.axis_index(n).astype(jnp.int32) for n in ("z", "x", "c", "exp"))
        tok_rows, width = tokens.shape
        scale = NROUTE / (TOP * tok_rows * A * B * C)
        local_experts, _, _ = whiten.shape
        hidden = deltas.shape[2]
        rank = basis.shape[1]
        shares = B if basis.shape[0] // (B * C) % (2 * 128) == 0 else 1
        share = x if shares > 1 else 0
        part_rows = basis.shape[0] // (shares * C)
        ka = rank // A
        col_width = width // E
        span = width // (A * B * C)
        sets = [list(range(0, A // 2)), list(range(A // 2, A))]
        spans = [slice(js[0] * ka, (js[-1] + 1) * ka) for js in sets]

        group_at = z * (B * C * span)
        first = group_at - y * col_width
        holder = (first >= 0) & (first + B * C * span <= col_width)
        scalars = [c, x, z, y, jnp.where(holder, first, 0)]
        for s in range(1, E):
            for t in range(shares):
                at = ((y + s) % E * shares + (share + t) % shares) * C
                scalars += [at + c, at + 1 - c]
        scalars = jnp.stack(scalars).astype(jnp.int32)

        w_rec = swap_core(whiten)
        d_rec = swap_core(deltas)

        def fetch(n, basis):
            cols = spans[n]
            mine = lax.dynamic_slice(
                basis, ((share * C + c) * part_rows, cols.start), (part_rows, cols.stop - cols.start)
            )
            got = []
            for s in range(1, E):
                got.append(shift_to(mine, "exp", -s % E, E))
            got = [jnp.concatenate(got) if len(got) > 1 else got[0]]
            got += [shift_to(got[0], "x", -t % B, B) for t in range(1, shares)]
            both = []
            for g in got:
                both += [g, swap_core(g)]
            if E == 2:
                return both
            return [g[s * part_rows : (s + 1) * part_rows] for s in range(E - 1) for g in both]

        fetched = [fetch(0, basis)]

        last_steps = [A // 2] if A > 2 else []
        first_steps = [m for m in reversed(range(1, A)) if m not in last_steps]

        def routed(g):
            hits = jnp.any(route_ids == g, axis=1)
            places = jnp.cumsum(hits.astype(jnp.int32)) - 1
            pick = (places[None, :] == jnp.arange(CAP)[:, None]) & hits[None, :]
            mine = lax.dynamic_slice_in_dim(tokens, y * col_width, col_width, 1)
            own = dot(pick.astype(BF), mine, ((1,), (0,))).astype(BF)
            nonlocal later
            own, later = lax.optimization_barrier((own, basis))
            early = [own]
            for m in first_steps:
                early.append(exchange(own, "z", m, A))
            late = []
            for m in last_steps:
                late.append(exchange(own, "z", m, A))
            early[1:] = in_hbm(*early[1:])
            feats = lax.dynamic_slice_in_dim(tokens, group_at, B * C * span, 1)
            turned = dot(feats, pick.astype(BF), ((0,), (1,))).astype(BF).reshape(B, C, span, CAP)
            mine = [lax.dynamic_index_in_dim(turned, (c + k) % C, 1, False).reshape(B * span, CAP) for k in range(C)]
            mine[1] = swap_core(mine[1])
            return ([early, late] if late else [early]), mine

        def gram_sends(groups):
            groups, mine = groups
            cols, rows, spots = [], [], []
            paired = E == 2 and col_width % (B * C * span) == 0
            for n, blocks in enumerate(groups):
                skip = int(n == 0 and paired and len(blocks) > 1)
                both, part = merge(scalars, blocks, B, span, skip)
                other = swap_core(both)
                if skip:
                    rows += mine
                    spots += [(len(cols), 0), (len(cols) + 1, 0)]
                if paired:
                    pairs = []
                    for a in range(A):
                        h = a * B * C * span // col_width
                        pairs.append((a * E + h, a * E + 1 - h))
                    got = lax.ppermute(part, ("z", "exp"), pairs)
                    part = jnp.where(holder, part, got)
                else:
                    every = lax.all_gather(both, "exp", axis=1, tiled=True)
                    near = lax.dynamic_slice_in_dim(every, group_at, B * C * span, 1).reshape(-1, B, C, span)
                    part = jnp.stack(
                        [lax.dynamic_index_in_dim(near, (c + k) % C, 2, False).reshape(-1, B * span).T for k in range(C)]
                    )
                rows += [part[0], swap_core(part[1])]
                at = skip * CAP
                spots += [(len(cols), at), (len(cols) + 1, at)]
                cols += [both, other]
            keeps, gots = [], []
            for first, steps in PIECES:
                keep, send = gram_part(scalars, cols, rows, spots, first, steps, col_width // TILES, B, span)
                gots.append([shift_to(send[s - 1], "x", s, B) for s in range(1, B)])
                keeps.append(keep)
            return keeps, gots

        local = local_part(scalars, whiten, w_rec, basis)

        later = basis
        routed_all = [routed(g) for g in range(GRAM_EXP)]
        fetched += [fetch(n, later) for n in range(1, len(spans))]
        grams = [gram_sends(r) for r in routed_all]

        coefs, lows, others = [], [], []
        for js, cols, got in zip(sets, spans, fetched):
            send, keep = chunk_product(
                scalars, whiten, w_rec, deltas, d_rec, local, got, cols.start // (cols.stop - cols.start), len(js), A, B
            )
            got_x = [shift_to(send[s - 1], "x", s, B) for s in range(1, B)]

            def at(a):
                out = lax.dynamic_index_in_dim(keep, a, 0, False)
                for r in got_x:
                    out = out + lax.dynamic_index_in_dim(r, a, 0, False).astype(F32)
                return out

            total = at(z)
            away = [at(partner(z, s, A)).astype(BF) for s in range(1, A)]
            for s in range(1, A):
                away[s - 1] = exchange(away[s - 1], "z", s, A)
            for blk in away:
                total = total + blk.astype(F32)
            coef = total.reshape(len(js), ka // B, hidden // A)
            coefs.append(coef)
            lows.append(coef.astype(BF))
            others.append([shift_to(lows[-1], "x", -s % B, B) for s in range(1, B)])
        mineh, away = product(scalars, lows, others, sets, A, B)
        away = swap_core(away)
        mineh = mineh + away.astype(F32)
        bg = lax.dynamic_index_in_dim(mineh, z, 0, False)
        for s in range(1, A):
            blk = lax.dynamic_index_in_dim(mineh, partner(z, s, A), 0, False).astype(BF)
            blk = exchange(blk, "z", s, A)
            bg = bg + blk.astype(F32)
        if E == 2:
            bg = bg.astype(BF)
            got = shift_to(bg, "exp", 1, E)
            bg = bg.astype(F32) + got.astype(F32)
        else:
            bg = lax.psum(bg, "exp")
        basis_gram = bg / (local_experts * E * hidden)

        coef = jnp.concatenate(coefs)
        blocks = [lax.dynamic_index_in_dim(coef, z, 0, False)]
        for s in range(1, A):
            blk = lax.dynamic_index_in_dim(coef, partner(z, s, A), 0, False).astype(BF)
            blocks.append(exchange(blk, "z", s, A))
        mine, other = own_rows(scalars, blocks, A)
        other = swap_core(other)
        coefficients = pair(scalars, mine, other)

        out = [finish(scalars, keeps, gots, scale) for keeps, gots in grams]
        return jnp.stack(out, 1), coefficients, basis_gram

    def named(*args):
        return shards(*args)

    return named, (A, B, C, E)


def solution(mesh):
    shards, (A, B, C, E) = build(mesh)
    fine = Mesh(mesh.devices.reshape(A, B, C, E), ("z", "x", "c", "exp"))
    tok = ("z", "x", "c")
    placed = (P(tok, None), P(tok, None), P("exp", tok, None), P("exp", tok, None), P("exp", None))
    return jax.shard_map(
        shards,
        mesh=fine,
        in_specs=placed,
        out_specs=(P(tok, None, "exp"), P(tok, "exp", None), P(tok, None)),
        check_vma=False,
    )
```
